256 devices in a mesh: wide: 32 (over x, y, core), narrow: 8 (over z).
Axes of the slice: x: 4, y: 4, z: 8, core: 2. Of those that a mesh axis runs over, the one named last changes fastest.
Arguments:
- blocks: bfloat16 [32, 8, 16, 64, 4096], P('wide', 'narrow'), may hold values from -16 to 16
- row_tile: int32 [32, 8, 16], P('wide', 'narrow'), may hold values from 0 to 15
- col_tile: int32 [32, 8, 16], P('wide', 'narrow'), may hold values from 0 to 63, as said below
- depth_tile: int32 [32, 8, 16], P('wide', 'narrow'), may hold values from 0 to 15
- block_count: int32 [32, 8], P('wide', 'narrow'), may hold values from 4 to 16, as said below
- factor_b: bfloat16 [32768, 256], P(('wide', 'narrow')), may hold values from -40 to 40
- factor_c: bfloat16 [1024, 256], replicated, may hold values from -0.076293945 to 0.076293945
Outputs:
- a_new: float32 [32768, 256], P(('wide', 'narrow'))
- b_new: float32 [32768, 256], P(('wide', 'narrow'))
The draws below stay inside these ranges and needn't reach their ends.
Inputs may be any that keep to these rules, and one draw needn't show every extreme that they name: `block_count`: every device holds at least 4 live blocks, and some device exactly 16. col_tile // 2 is the index of wide that holds the block's mode-2 factor rows; among the 16 slots of one device, live or not, each such index appears at most 1 times, and some index exactly 1 times.
All inputs are finite; a program needn't handle non-finite values.
Results may differ from the reference program's by a relative error of at most 0.02.
Values may be sent and summed in bfloat16 or wider, within the bound.
No kernel may reach another device: no remote copies, remote signals or barrier semaphores. Data moves between devices by JAX's collectives and lax.ppermute only.
A program may use at most 128 MiB of HBM per device.

```python
import jax
import jax.numpy as jnp
from jax import lax

R = 256
BS = 64
TI_DEV = 2
TJ_DEV = 2
NTK = 16
CAP = 16
SLOTS = 1
NI = 32768
NJ = 32768
N_WIDE = 32
N_NARROW = 8


def draw_blocks(key, part):
    key_core, key_scale = jax.random.split(key)
    shape = (N_WIDE, N_NARROW, CAP, BS, BS * BS)
    wide_pos = jnp.arange(N_WIDE, dtype=jnp.float32) / max(N_WIDE - 1, 1)
    trend = (2.0 * jnp.exp(jnp.log(12.0) * (wide_pos - 1.0))).reshape(N_WIDE, 1, 1, 1, 1)
    scale_draw = jax.random.uniform(key_scale, (N_WIDE, N_NARROW, CAP, 1, 1), jnp.float32)
    core = jnp.clip(jax.random.normal(key_core, shape, jnp.float32), -6.0, 6.0)
    block_scale = jnp.exp(jnp.log(3.0) * (scale_draw - 0.5))
    return jnp.clip(core * trend * block_scale, -16.0, 16.0).astype(jnp.bfloat16)


def draw_block_count(key, part):
    key_base, key_full = jax.random.split(key)
    total_devices = N_WIDE * N_NARROW
    low_count = max(1, CAP // 4)
    high_count = max(low_count + 1, CAP)
    base_counts = jax.random.randint(key_base, (total_devices,), low_count, high_count, dtype=jnp.int32)
    fuller = jax.random.randint(key_full, (), 0, total_devices, dtype=jnp.int32)
    counts = jnp.where(jnp.arange(total_devices, dtype=jnp.int32) == fuller, CAP, base_counts)
    return counts.reshape(N_WIDE, N_NARROW).astype(jnp.int32)


def draw_col_tile(key, part):
    key_perm, key_local = jax.random.split(key)
    total_devices = N_WIDE * N_NARROW
    device_keys = jax.random.split(key_perm, total_devices)
    picks = jax.vmap(lambda one_key: jax.random.permutation(one_key, N_WIDE * SLOTS)[:CAP])(device_keys)
    owners = picks.astype(jnp.int32) % N_WIDE
    inside = jax.random.randint(key_local, (total_devices, CAP), 0, TJ_DEV, dtype=jnp.int32)
    return (owners * TJ_DEV + inside).reshape(N_WIDE, N_NARROW, CAP).astype(jnp.int32)


def pair_plan(key):
    plan_key = jax.random.fold_in(key, 4099)
    key_perm, key_depth = jax.random.split(plan_key)
    column_order = jax.random.permutation(key_perm, R).astype(jnp.int32)
    positions = jnp.arange(R, dtype=jnp.int32)
    partner = jnp.zeros((R,), jnp.int32).at[column_order].set(column_order[jnp.bitwise_xor(positions, 1)])
    leader = jnp.zeros((R,), jnp.int32).at[column_order].set(1 - positions % 2)
    pair_id = jnp.zeros((R,), jnp.int32).at[column_order].set(positions // 2)
    depth_draw = jax.random.uniform(key_depth, (R // 2,), jnp.float32)
    residue = jnp.exp(jnp.log(0.002) * depth_draw)
    return (partner, leader, jnp.take(residue, pair_id), pair_id)


def factor_body(key, rows, bound, plan, boost):
    key_core, key_shift, key_spread, key_column = jax.random.split(key, 4)
    position = jnp.arange(rows, dtype=jnp.float32) / rows
    trend = (0.5 * (1.0 + 2.0 * position)).reshape(rows, 1)
    spread_draw = jax.random.uniform(key_spread, (rows, 1), jnp.float32)
    column_draw = jax.random.uniform(key_column, (1, R), jnp.float32)
    core = jnp.clip(jax.random.normal(key_core, (rows, R), jnp.float32), -6.0, 6.0)
    column_shift = jax.random.uniform(key_shift, (1, R), jnp.float32, -0.6, 0.6)
    spread = jnp.exp(jnp.log(10.0) * (spread_draw - 0.5))
    column_scale = jnp.exp(bound * (column_draw - 0.5))
    values = (core + column_shift) * spread * trend * boost
    partner, leader, residue, pair_id = plan
    partner_values = jnp.take(values, partner, axis=1)
    follower = jnp.sqrt(1.0 - residue)[None, :] * partner_values + jnp.sqrt(residue)[None, :] * values
    mixed = jnp.where(leader[None, :] > 0, values, follower)
    return (mixed, column_scale)


def draw_factor_b(key, part):
    rows = TJ_DEV * N_WIDE * N_NARROW * BS
    total_devices = N_WIDE * N_NARROW
    plan = pair_plan(key)
    pair_id = plan[3]
    half_rank = R // 2
    pair_order = jax.random.permutation(jax.random.fold_in(key, 21), half_rank).astype(jnp.int32)
    device_ids = jnp.arange(total_devices, dtype=jnp.int32)
    heavy_pair = jnp.take(pair_order, device_ids % half_rank)
    boosted = (device_ids // half_rank % 4 == 0).astype(jnp.float32)
    hit = (heavy_pair[:, None] == pair_id[None, :]).astype(jnp.float32)
    boost_dev = 1.0 + 7.0 * hit * boosted[:, None]
    boost = jnp.repeat(boost_dev, TJ_DEV * BS, axis=0)
    values, column_scale = factor_body(jax.random.fold_in(key, 11), rows, 0.0, plan, boost)
    return jnp.clip(values, -40.0, 40.0).astype(jnp.bfloat16)


def draw_factor_c(key, part):
    rows = NTK * BS
    gamma = 1.0 / (TJ_DEV * N_WIDE * N_NARROW * NTK * BS)
    plan = pair_plan(key)
    lift = (1.0 / plan[2]).reshape(1, R)
    values, column_scale = factor_body(jax.random.fold_in(key, 12), rows, jnp.log(4.0), plan, 1.0)
    return (jnp.clip(values * column_scale * lift, -40000.0, 40000.0) * gamma).astype(jnp.bfloat16)


def plant(result, key, low, high):
    place = [jax.random.randint(jax.random.fold_in(key, axis), (), 0, length) for axis, length in enumerate(result.shape)]
    widest = result.shape.index(max(result.shape))
    beside = place[:widest] + [(place[widest] + 1) % result.shape[widest]] + place[widest + 1:]
    return result.at[tuple(place)].set(low).at[tuple(beside)].set(high)


def setup_inputs(seed: int = 0) -> dict:
    splits = jax.random.split(jax.random.key(seed), 8)
    return {
        "blocks": draw_blocks(jax.random.fold_in(splits[7], 71), 0),
        "row_tile": plant(jax.random.randint(splits[1], (N_WIDE, N_NARROW, CAP), 0, N_NARROW * TI_DEV), jax.random.fold_in(splits[1], 1), 0, (N_NARROW * TI_DEV) - 1).astype(jnp.int32),
        "col_tile": draw_col_tile(jax.random.fold_in(splits[7], 71), 0),
        "depth_tile": plant(jax.random.randint(splits[3], (N_WIDE, N_NARROW, CAP), 0, NTK), jax.random.fold_in(splits[3], 1), 0, NTK - 1).astype(jnp.int32),
        "block_count": draw_block_count(jax.random.fold_in(splits[7], 71), 0),
        "factor_b": draw_factor_b(jax.random.fold_in(splits[7], 71), 0),
        "factor_c": draw_factor_c(jax.random.fold_in(splits[7], 71), 0),
    }


def right_solve(target, matrix):
    chol_lower = jnp.linalg.cholesky(matrix)
    middle = lax.linalg.triangular_solve(chol_lower, target, left_side=False, lower=True, transpose_a=True)
    return lax.linalg.triangular_solve(chol_lower, middle, left_side=False, lower=True, transpose_a=False)

def depth_mix(one_block, depth_id, factor_c):
    depth_rows = lax.dynamic_slice_in_dim(factor_c, depth_id * BS, BS, 0)
    depth_mixed = lax.dot_general(one_block.astype(jnp.float32), depth_rows.astype(jnp.float32), (((0,), (0,)), ((), ())), preferred_element_type=jnp.float32)
    return depth_mixed.reshape(BS, BS, depth_rows.shape[1])

def flatten(values):
    return values.reshape(-1).astype(jnp.int32)

def reference(blocks, row_tile, col_tile, depth_tile, block_count, factor_b, factor_c):
    rank_width = factor_c.shape[1]
    slot_ids = jnp.arange(CAP, dtype=jnp.int32)
    wide_ids = jnp.arange(N_WIDE, dtype=jnp.int32)[:, None, None]
    narrow_ids = jnp.arange(N_NARROW, dtype=jnp.int32)[None, :, None]
    alive_mask = (slot_ids[None, None, :] < block_count[:, :, None]).astype(jnp.int32)
    first_tile = wide_ids * (N_NARROW * TI_DEV) + row_tile
    owners = col_tile // TJ_DEV
    second_tile = (owners * N_NARROW + narrow_ids) * TJ_DEV + col_tile % TJ_DEV
    scan_items = (blocks.reshape(-1, BS, BS * BS), flatten(first_tile), flatten(second_tile), flatten(depth_tile), flatten(alive_mask))
    gram_c = jnp.dot(factor_c.T.astype(jnp.float32), factor_c.astype(jnp.float32), preferred_element_type=jnp.float32)
    gram_b = jnp.dot(factor_b.T.astype(jnp.float32), factor_b.astype(jnp.float32), preferred_element_type=jnp.float32)

    def first_pass(partial_sum, item):
        one_block, first_id, second_id, depth_id, alive = item

        def add_block(running):
            depth_mixed = depth_mix(one_block, depth_id, factor_c)
            b_rows = lax.dynamic_slice_in_dim(factor_b, second_id * BS, BS, 0).astype(jnp.float32)
            b_term = jnp.sum(depth_mixed * b_rows[None, :, :], axis=1)
            current = lax.dynamic_slice_in_dim(running, first_id * BS, BS, 0)
            return lax.dynamic_update_slice_in_dim(running, current + b_term, first_id * BS, 0)
        return (lax.cond(alive > 0, add_block, lambda running: running, partial_sum), None)
    mttkrp_a, _ = lax.scan(first_pass, jnp.zeros((NI, rank_width), jnp.float32), scan_items)
    a_new = right_solve(mttkrp_a, gram_b * gram_c)
    a_half = a_new.astype(jnp.bfloat16)
    gram_a = jnp.dot(a_half.T.astype(jnp.float32), a_half.astype(jnp.float32), preferred_element_type=jnp.float32)

    def second_pass(partial_sum, item):
        one_block, first_id, second_id, depth_id, alive = item

        def add_block(running):
            depth_mixed = depth_mix(one_block, depth_id, factor_c)
            a_part = lax.dynamic_slice_in_dim(a_half, first_id * BS, BS, 0).astype(jnp.float32)
            a_term = jnp.sum(depth_mixed * a_part[:, None, :], axis=0)
            current = lax.dynamic_slice_in_dim(running, second_id * BS, BS, 0)
            return lax.dynamic_update_slice_in_dim(running, current + a_term, second_id * BS, 0)
        return (lax.cond(alive > 0, add_block, lambda running: running, partial_sum), None)
    mttkrp_b, _ = lax.scan(second_pass, jnp.zeros((NJ, rank_width), jnp.float32), scan_items)
    b_new = right_solve(mttkrp_b, gram_a * gram_c)
    return (a_new, b_new)
```

```python
import functools

import jax
import jax.numpy as jnp
from jax import lax
from jax.experimental import pallas as pl
from jax.experimental.pallas import tpu as pltpu
from jax.sharding import PartitionSpec as P

TI_DEV = 2
TJ_DEV = 2
NX = 4
NY = 4
NC = 2
HI = lax.Precision.HIGHEST
CHUNK = 8


def flat_wide(x, y, c):
    return ((x % NX) * NY + (y % NY)) * NC + c


def shift_wide(v, dx, dy, dc):
    pairs = []
    for x in range(NX):
        for y in range(NY):
            for c in range(NC):
                pairs.append((flat_wide(x, y, c), flat_wide(x + dx, y + dy, c ^ dc)))
    return lax.ppermute(v, "wide", pairs)


def xor_wide(v, bx, by):
    pairs = []
    for x in range(NX):
        for y in range(NY):
            for c in range(NC):
                pairs.append((flat_wide(x, y, c), flat_wide(x ^ bx, y ^ by, c)))
    return lax.ppermute(v, "wide", pairs)


def column_gram(matrix):
    return lax.dot_general(
        matrix, matrix, (((0,), (0,)), ((), ())), preferred_element_type=jnp.float32
    )


def pass_one_kernel(rows_ref, picks_ref, depth_ref, count_ref, x_ref, b_ref, c_ref, out_ref):
    slot = pl.program_id(0)
    bs = b_ref.shape[1]

    @pl.when(slot == 0)
    def _():
        out_ref[...] = jnp.zeros_like(out_ref)

    @pl.when(slot < count_ref[0])
    def _():
        c_rows = c_ref[pl.ds(pl.multiple_of(depth_ref[slot] * bs, bs), bs), :]
        b_rows = b_ref[0].astype(jnp.float32)
        target = rows_ref[slot]
        for k in range(bs // CHUNK):
            part = x_ref[0, :, k * CHUNK * bs:(k + 1) * CHUNK * bs]
            mixed = lax.dot_general(
                part, c_rows, (((0,), (0,)), ((), ())), preferred_element_type=jnp.float32
            )
            mixed = mixed.reshape(CHUNK, bs, mixed.shape[-1])
            term = jnp.sum(mixed * b_rows[None, :, :], axis=1)
            out_ref[target, k * CHUNK:(k + 1) * CHUNK, :] += term


def pass_two_kernel(picks_ref, owners_ref, depth_ref, count_ref, x_ref, a_ref, c_ref, out_ref):
    slot = pl.program_id(0)
    bs = a_ref.shape[1]

    @pl.when(slot == 0)
    def _():
        out_ref[...] = jnp.zeros_like(out_ref)

    @pl.when(slot < count_ref[0])
    def _():
        c_rows = c_ref[pl.ds(pl.multiple_of(depth_ref[slot] * bs, bs), bs), :]
        total = jnp.zeros((bs, c_rows.shape[-1]), jnp.float32)
        for k in range(bs // CHUNK):
            part = x_ref[0, :, k * CHUNK * bs:(k + 1) * CHUNK * bs]
            mixed = lax.dot_general(
                part, c_rows, (((0,), (0,)), ((), ())), preferred_element_type=jnp.float32
            )
            mixed = mixed.reshape(CHUNK, bs, mixed.shape[-1])
            a_rows = a_ref[0, k * CHUNK:(k + 1) * CHUNK, :].astype(jnp.float32)
            total = total + jnp.sum(mixed * a_rows[:, None, :], axis=0)
        out_ref[owners_ref[slot]] = total


def run_pass(kernel, first, second, depth, count, blocks, tiles, factor_c, out_tiles, use_first):
    slots, bs, wide_block = blocks.shape
    rank = factor_c.shape[1]

    def live(s, cnt):
        return jnp.minimum(s, cnt[0] - 1)

    def tile_map(s, f, p, d, cnt):
        table = f if use_first else p
        return (table[live(s, cnt)], 0, 0)

    return pl.pallas_call(
        kernel,
        out_shape=jax.ShapeDtypeStruct((out_tiles, bs, rank), jnp.float32),
        grid_spec=pltpu.PrefetchScalarGridSpec(
            num_scalar_prefetch=4,
            grid=(slots,),
            in_specs=[
                pl.BlockSpec((1, bs, wide_block), lambda s, f, p, d, cnt: (live(s, cnt), 0, 0)),
                pl.BlockSpec((1, bs, rank), tile_map),
                pl.BlockSpec(factor_c.shape, lambda s, f, p, d, cnt: (0, 0)),
            ],
            out_specs=pl.BlockSpec((out_tiles, bs, rank), lambda s, f, p, d, cnt: (0, 0, 0)),
        ),
        compiler_params=pltpu.CompilerParams(dimension_semantics=("arbitrary",)),
        cost_estimate=pl.CostEstimate(
            flops=slots * wide_block * bs * rank * 2,
            bytes_accessed=slots * bs * wide_block * 2,
            transcendentals=0,
        ),
    )(first, second, depth, count, blocks, tiles, factor_c)


def mm(a, b, dims=((1,), (0,))):
    return lax.dot_general(a, b, (dims, ((), ())), precision=HI, preferred_element_type=jnp.float32)


def sweep_inverse(ref):
    n = ref.shape[0]
    row_ids = lax.broadcasted_iota(jnp.int32, (n, n), 0)
    lane_ids = lax.broadcasted_iota(jnp.int32, (n, n), 1)

    def step(k, carry):
        a = ref[...]
        row = ref[pl.ds(k, 1), :]
        lane = lane_ids == k
        col = jnp.sum(jnp.where(lane, a, 0.0), axis=1, keepdims=True)
        pivot = jnp.sum(jnp.where(lane[:1], row, 0.0), axis=1, keepdims=True)
        inv = 1.0 / pivot
        row_p = jnp.where(lane[:1], inv, row * inv)
        cleared = jnp.where(lane, 0.0, a)
        ref[...] = jnp.where(row_ids == k, row_p, cleared - col * row_p)
        return carry

    lax.fori_loop(0, n, step, 0)


def invert_kernel(g_ref, c_ref, scale_ref, a1_ref, t_ref, s1_ref):
    rank = g_ref.shape[0]
    half = rank // 2
    g = g_ref[...] * c_ref[...]
    eye = (
        lax.broadcasted_iota(jnp.int32, (rank, rank), 0)
        == lax.broadcasted_iota(jnp.int32, (rank, rank), 1)
    )
    diag = jnp.where(eye, g, 0.0)
    d_row = lax.rsqrt(jnp.sum(diag, axis=0, keepdims=True))
    d_col = lax.rsqrt(jnp.sum(diag, axis=1, keepdims=True))
    scale_ref[...] = d_row
    g = g * d_row * d_col
    a1_ref[...] = g[:half, :half]
    sweep_inverse(a1_ref)
    b = g[half:, :half]
    t = mm(b, a1_ref[...])
    t_ref[...] = t
    s1_ref[...] = g[half:, half:] - mm(t, b, ((1,), (1,)))
    sweep_inverse(s1_ref)


def invert(gram, gram_c):
    rank = gram.shape[0]
    half = rank // 2
    sq = jax.ShapeDtypeStruct((half, half), jnp.float32)
    return pl.pallas_call(
        invert_kernel,
        out_shape=(jax.ShapeDtypeStruct((1, rank), jnp.float32), sq, sq, sq),
        cost_estimate=pl.CostEstimate(flops=10**10, bytes_accessed=10**6, transcendentals=0),
    )(gram, gram_c)


def apply_inverse(m, scale_ref, a1_ref, t_ref, s1_ref):
    half = a1_ref.shape[0]
    m = m * scale_ref[...]
    m1 = m[:, :half]
    z2 = mm(m[:, half:] - mm(m1, t_ref[...], ((1,), (1,))), s1_ref[...])
    z1 = mm(m1, a1_ref[...]) - mm(z2, t_ref[...])
    return jnp.concatenate([z1, z2], axis=1) * scale_ref[...]


def apply_first_kernel(m_ref, scale_ref, a1_ref, t_ref, s1_ref, out_ref, half_ref):
    m = m_ref[0]
    for k in range(1, m_ref.shape[0]):
        m = m + m_ref[k]
    z = apply_inverse(m, scale_ref, a1_ref, t_ref, s1_ref)
    out_ref[...] = z
    half_ref[...] = z.astype(jnp.bfloat16)


def apply_second_kernel(flags_ref, m_ref, scale_ref, a1_ref, t_ref, s1_ref, out_ref, acc_ref):
    acc_ref[...] = jnp.zeros_like(acc_ref)

    def step(k, carry):
        acc_ref[flags_ref[k]] += m_ref[k]
        return carry

    lax.fori_loop(0, m_ref.shape[0], step, 0)
    m = acc_ref[...].reshape(out_ref.shape)
    out_ref[...] = apply_inverse(m, scale_ref, a1_ref, t_ref, s1_ref)


def roll_blocks(parts, offset):
    stacked = jnp.concatenate(parts + parts, axis=0)
    rows = parts[0].shape[0]
    return lax.dynamic_slice_in_dim(stacked, offset * rows, rows * len(parts), 0)


def gather_slices(piece, x, c):
    parts = [shift_wide(piece, 3, 0, 0), shift_wide(piece, 2, 0, 0), shift_wide(piece, 1, 0, 0), piece]
    mine = roll_blocks(parts, (3 - x) % NX)
    other = shift_wide(mine, 0, 0, 1)
    return jnp.concatenate(
        [jnp.where(c == 0, mine, other), jnp.where(c == 0, other, mine)], axis=0
    )


def local(blocks, row_tile, col_tile, depth_tile, block_count, factor_b, factor_c):
    local_blocks = blocks[0, 0]
    first_ids = row_tile[0, 0]
    second_ids = col_tile[0, 0]
    depth_ids = depth_tile[0, 0]
    count = block_count[0]
    bs = local_blocks.shape[1]
    rank = factor_c.shape[1]
    n_wide = lax.axis_size("wide")
    n_narrow = lax.axis_size("narrow")
    rows = factor_b.shape[0]
    w = lax.axis_index("wide")
    n = lax.axis_index("narrow")
    x = w // (NY * NC)
    y = (w // NC) % NY
    c = w % NC
    owners = second_ids // TJ_DEV
    inside = second_ids % TJ_DEV

    gram_c = column_gram(factor_c)

    flags = jnp.sum(
        jnp.where(owners[:, None] == jnp.arange(rank, dtype=jnp.int32)[None, :], inside[:, None], 0),
        axis=0,
    )
    flag_rows = jnp.broadcast_to(flags.astype(jnp.bfloat16)[None, :], (16, rank))
    packed = jnp.concatenate([factor_b, flag_rows], axis=0)[None]
    along_x = jnp.concatenate([packed] + [shift_wide(packed, k, 0, 0) for k in (1, 2, 3)], axis=0)
    along_y = jnp.concatenate([along_x] + [shift_wide(along_x, 0, k, 0) for k in (1, 2, 3)], axis=0)
    gathered = jnp.concatenate([along_y, shift_wide(along_y, 0, 0, 1)], axis=0)
    b_rows = gathered[:, :rows]

    def relative(owner):
        ox = owner // (NY * NC)
        oy = (owner // NC) % NY
        oc = owner % NC
        return ((c ^ oc) * NY + (y - oy) % NY) * NX + (x - ox) % NX

    mine = (jnp.arange(rank, dtype=jnp.int32) == w).astype(jnp.float32)
    flags_rel = jnp.sum(gathered[:, rows].astype(jnp.float32) * mine[None, :], axis=1).astype(jnp.int32)
    flags_abs = jnp.take(flags_rel, relative(jnp.arange(n_wide, dtype=jnp.int32)))

    b_tiles = b_rows.reshape(n_wide * TJ_DEV, bs, rank)
    b_pick = relative(owners) * TJ_DEV + inside

    gram_plane = column_gram(b_rows.reshape(n_wide * rows, rank))
    quarter = rank // (NC * NX)
    piece = lax.dynamic_slice_in_dim(gram_plane, (c * NX + x) * quarter, quarter, 0)
    for d in (1, 2, 4):
        piece = piece + lax.ppermute(piece, "narrow", [(i, i ^ d) for i in range(n_narrow)])
    gram_b = gather_slices(piece, x, c)

    first_part = run_pass(
        pass_one_kernel, first_ids, b_pick, depth_ids, count, local_blocks, b_tiles, factor_c,
        n_narrow * TI_DEV, False,
    )
    received = lax.all_to_all(
        first_part.reshape(n_narrow, TI_DEV * bs, rank), "narrow", 0, 0, tiled=True
    )
    factors = invert(gram_b, gram_c)
    out = jax.ShapeDtypeStruct((rows, rank), jnp.float32)
    a_new, a_half = pl.pallas_call(
        apply_first_kernel, out_shape=(out, jax.ShapeDtypeStruct((rows, rank), jnp.bfloat16))
    )(received, *factors)

    a_all = jnp.stack(
        [a_half]
        + [
            lax.ppermute(a_half, "narrow", [(i, (i + k) % n_narrow) for i in range(n_narrow)])
            for k in range(1, n_narrow)
        ]
    )
    a_tiles = a_all.reshape(n_narrow * TI_DEV, bs, rank)
    a_pick = ((n - first_ids // TI_DEV) % n_narrow) * TI_DEV + first_ids % TI_DEV

    gram_w = column_gram(a_all.reshape(n_narrow * rows, rank))
    half = rank // NC
    keep = lax.dynamic_slice_in_dim(gram_w, c * half, half, 0)
    give = lax.dynamic_slice_in_dim(gram_w, (1 - c) * half, half, 0)
    keep = keep + shift_wide(give, 0, 0, 1)
    piece = lax.dynamic_slice_in_dim(keep, x * quarter, quarter, 0)
    for k in (1, 2, 3):
        give = lax.dynamic_slice_in_dim(keep, ((x + k) % NX) * quarter, quarter, 0)
        piece = piece + shift_wide(give, k, 0, 0)
    for d in (1, 2):
        piece = piece + xor_wide(piece, 0, d)
    gram_a = gather_slices(piece, x, c)

    second_part = run_pass(
        pass_two_kernel, a_pick, owners, depth_ids, count, local_blocks, a_tiles, factor_c,
        n_wide, True,
    )
    received_b = lax.all_to_all(second_part, "wide", 0, 0, tiled=True)
    factors_b = invert(gram_a, gram_c)
    vmem = pl.BlockSpec(memory_space=pltpu.VMEM)
    b_new = pl.pallas_call(
        apply_second_kernel,
        out_shape=out,
        in_specs=[pl.BlockSpec(memory_space=pltpu.SMEM)] + [vmem] * 5,
        out_specs=vmem,
        scratch_shapes=[pltpu.VMEM((TJ_DEV, bs, rank), jnp.float32)],
    )(flags_abs, received_b, *factors_b)
    return (a_new, b_new)


def solution(mesh):
    return jax.shard_map(
        local,
        mesh=mesh,
        in_specs=(
            P("wide", "narrow", None, None, None),
            P("wide", "narrow", None),
            P("wide", "narrow", None),
            P("wide", "narrow", None),
            P("wide", "narrow"),
            P(("wide", "narrow"), None),
            P(),
        ),
        out_specs=(P(("wide", "narrow"), None), P(("wide", "narrow"), None)),
        check_vma=False,
    )
```

```python
import functools

import jax
import jax.numpy as jnp
from jax import lax
from jax.experimental import pallas as pl
from jax.experimental.pallas import tpu as pltpu
from jax.sharding import PartitionSpec as P

TI_DEV = 2
TJ_DEV = 2
NX = 4
NY = 4
NC = 2
HI = lax.Precision.HIGHEST
CHUNK = 8
PANEL = 8
PIECES = 2


def flat_wide(x, y, c):
    return ((x % NX) * NY + (y % NY)) * NC + c


def shift_wide(v, dx, dy, dc):
    pairs = []
    for x in range(NX):
        for y in range(NY):
            for c in range(NC):
                pairs.append((flat_wide(x, y, c), flat_wide(x + dx, y + dy, c ^ dc)))
    return lax.ppermute(v, "wide", pairs)


def column_gram(matrix):
    return lax.dot_general(
        matrix, matrix, (((0,), (0,)), ((), ())), preferred_element_type=jnp.float32
    )


def begin(slot, first, previous, out_ref):
    @pl.when(slot == first)
    def _():
        out_ref[...] = previous[0][...] if previous else jnp.zeros_like(out_ref)


def pass_one_kernel(first, rows_ref, picks_ref, depth_ref, count_ref, x_ref, b_ref, c_ref, *rest):
    *previous, out_ref = rest
    slot = pl.program_id(0) + first
    bs = b_ref.shape[1]
    begin(slot, first, previous, out_ref)

    @pl.when(slot < count_ref[0])
    def _():
        c_rows = c_ref[pl.ds(pl.multiple_of(depth_ref[slot] * bs, bs), bs), :]
        b_rows = b_ref[0].astype(jnp.float32)
        target = rows_ref[slot]
        for k in range(bs // CHUNK):
            part = x_ref[0, :, k * CHUNK * bs:(k + 1) * CHUNK * bs]
            mixed = lax.dot_general(
                part, c_rows, (((0,), (0,)), ((), ())), preferred_element_type=jnp.float32
            )
            mixed = mixed.reshape(CHUNK, bs, mixed.shape[-1])
            term = jnp.sum(mixed * b_rows[None, :, :], axis=1)
            out_ref[target, k * CHUNK:(k + 1) * CHUNK, :] += term


def pass_two_kernel(first, picks_ref, owners_ref, depth_ref, count_ref, x_ref, a_ref, c_ref, *rest):
    *previous, out_ref = rest
    slot = pl.program_id(0) + first
    bs = a_ref.shape[1]
    begin(slot, first, previous, out_ref)

    @pl.when(slot < count_ref[0])
    def _():
        c_rows = c_ref[pl.ds(pl.multiple_of(depth_ref[slot] * bs, bs), bs), :]
        total = jnp.zeros((bs, c_rows.shape[-1]), jnp.float32)
        for k in range(bs // CHUNK):
            part = x_ref[0, :, k * CHUNK * bs:(k + 1) * CHUNK * bs]
            mixed = lax.dot_general(
                part, c_rows, (((0,), (0,)), ((), ())), preferred_element_type=jnp.float32
            )
            mixed = mixed.reshape(CHUNK, bs, mixed.shape[-1])
            a_rows = a_ref[0, k * CHUNK:(k + 1) * CHUNK, :].astype(jnp.float32)
            total = total + jnp.sum(mixed * a_rows[:, None, :], axis=0)
        out_ref[owners_ref[slot]] = total


def run_pass(kernel, piece, tables, blocks, tiles, factor_c, out_tiles, use_first, previous=None):
    slots, bs, wide_block = blocks.shape
    rank = factor_c.shape[1]
    steps = slots // PIECES
    first = piece * steps
    extra = [] if previous is None else [previous]

    def live(s, cnt):
        return jnp.minimum(s + first, cnt[0] - 1)

    def tile_map(s, f, p, d, cnt):
        pick = (f if use_first else p)[live(s, cnt)]
        return (pick // TJ_DEV, pick % TJ_DEV, 0)

    whole = pl.BlockSpec((out_tiles, bs, rank), lambda s, f, p, d, cnt: (0, 0, 0))
    return pl.pallas_call(
        functools.partial(kernel, first),
        out_shape=jax.ShapeDtypeStruct((out_tiles, bs, rank), jnp.float32),
        grid_spec=pltpu.PrefetchScalarGridSpec(
            num_scalar_prefetch=4,
            grid=(steps,),
            in_specs=[
                pl.BlockSpec((1, bs, wide_block), lambda s, f, p, d, cnt: (live(s, cnt), 0, 0)),
                pl.BlockSpec((1, bs, rank), tile_map),
                pl.BlockSpec(factor_c.shape, lambda s, f, p, d, cnt: (0, 0)),
            ] + [whole] * len(extra),
            out_specs=whole,
        ),
        compiler_params=pltpu.CompilerParams(dimension_semantics=("arbitrary",)),
        cost_estimate=pl.CostEstimate(
            flops=steps * wide_block * bs * rank * 2,
            bytes_accessed=steps * bs * wide_block * 2,
            transcendentals=0,
        ),
    )(*tables, blocks, tiles, factor_c, *extra)


def mm(a, b, dims=((1,), (0,))):
    return lax.dot_general(a, b, (dims, ((), ())), precision=HI, preferred_element_type=jnp.float32)


def sweep_negated_inverse(ref):
    n = ref.shape[0]
    lane = lax.broadcasted_iota(jnp.int32, (n, n), 1)
    lane_p = lax.broadcasted_iota(jnp.int32, (PANEL, n), 1)
    sub_p = lax.broadcasted_iota(jnp.int32, (PANEL, n), 0)
    sub_1 = lax.broadcasted_iota(jnp.int32, (PANEL, 1), 0)

    def step(block, carry):
        start = pl.multiple_of(block * PANEL, PANEL)
        a = ref[...]
        panel = ref[pl.ds(start, PANEL), :]
        cols = []
        diag = []
        for j in range(PANEL):
            cols.append(jnp.sum(jnp.where(lane == start + j, a, 0.0), axis=1, keepdims=True))
            diag.append(jnp.sum(jnp.where(lane_p == start + j, panel, 0.0), axis=1, keepdims=True))
        for j in range(PANEL):
            here = lane_p == start + j
            inv = 1.0 / diag[j][j:j + 1]
            row = jnp.where(here[:1], inv, panel[j:j + 1] * inv)
            panel = jnp.where(sub_p == j, row, jnp.where(here, 0.0, panel) - diag[j] * row)
            for m in range(j + 1, PANEL):
                entry = diag[m][j:j + 1] * inv
                diag[m] = jnp.where(sub_1 == j, entry, diag[m] - diag[j] * entry)
        panel = jnp.where((lane_p >= start) & (lane_p < start + PANEL), -panel, panel)
        a = jnp.where((lane >= start) & (lane < start + PANEL), 0.0, a)
        for j in range(PANEL):
            a = a - cols[j] * panel[j:j + 1]
        ref[...] = a
        ref[pl.ds(start, PANEL), :] = panel
        return carry

    lax.fori_loop(0, n // PANEL, step, 0)
    ref[...] = -ref[...]


def invert_kernel(g_ref, c_ref, scale_ref, a1_ref, t_ref, s1_ref):
    rank = g_ref.shape[0]
    half = rank // 2
    g = g_ref[...] * c_ref[...]
    eye = (
        lax.broadcasted_iota(jnp.int32, (rank, rank), 0)
        == lax.broadcasted_iota(jnp.int32, (rank, rank), 1)
    )
    diag = jnp.where(eye, g, 0.0)
    d_row = lax.rsqrt(jnp.sum(diag, axis=0, keepdims=True))
    d_col = lax.rsqrt(jnp.sum(diag, axis=1, keepdims=True))
    scale_ref[...] = d_row
    g = g * d_row * d_col
    a1_ref[...] = g[:half, :half]
    sweep_negated_inverse(a1_ref)
    b = g[half:, :half]
    t = mm(b, a1_ref[...])
    t_ref[...] = t
    s1_ref[...] = g[half:, half:] - mm(t, b, ((1,), (1,)))
    sweep_negated_inverse(s1_ref)


def invert(gram, gram_c):
    rank = gram.shape[0]
    half = rank // 2
    sq = jax.ShapeDtypeStruct((half, half), jnp.float32)
    return pl.pallas_call(
        invert_kernel,
        out_shape=(jax.ShapeDtypeStruct((1, rank), jnp.float32), sq, sq, sq),
        cost_estimate=pl.CostEstimate(flops=10**10, bytes_accessed=10**6, transcendentals=0),
    )(gram, gram_c)


def apply_inverse(m, scale_ref, a1_ref, t_ref, s1_ref):
    half = a1_ref.shape[0]
    m = m * scale_ref[...]
    m1 = m[:, :half]
    z2 = mm(m[:, half:] - mm(m1, t_ref[...], ((1,), (1,))), s1_ref[...])
    z1 = mm(m1, a1_ref[...]) - mm(z2, t_ref[...])
    return jnp.concatenate([z1, z2], axis=1) * scale_ref[...]


def apply_first_kernel(m_ref, scale_ref, a1_ref, t_ref, s1_ref, out_ref, half_ref):
    m = m_ref[0]
    for k in range(1, m_ref.shape[0]):
        m = m + m_ref[k]
    z = apply_inverse(m, scale_ref, a1_ref, t_ref, s1_ref)
    out_ref[...] = z
    half_ref[...] = z.astype(jnp.bfloat16)


def apply_second_kernel(flags_ref, m_ref, scale_ref, a1_ref, t_ref, s1_ref, out_ref, acc_ref):
    acc_ref[...] = jnp.zeros_like(acc_ref)

    def step(k, carry):
        acc_ref[flags_ref[k]] += m_ref[k]
        return carry

    lax.fori_loop(0, m_ref.shape[0], step, 0)
    m = acc_ref[...].reshape(out_ref.shape)
    out_ref[...] = apply_inverse(m, scale_ref, a1_ref, t_ref, s1_ref)


def exchange(parts, axis):
    return lax.all_to_all(parts, axis, 0, 0, tiled=True)


def spread(piece, count, axis):
    return exchange(jnp.broadcast_to(piece[None], (count, *piece.shape)), axis)


def local(blocks, row_tile, col_tile, depth_tile, block_count, factor_b, factor_c):
    local_blocks = blocks[0, 0]
    first_ids = row_tile[0, 0]
    second_ids = col_tile[0, 0]
    depth_ids = depth_tile[0, 0]
    count = block_count[0]
    bs = local_blocks.shape[1]
    rank = factor_c.shape[1]
    n_wide = lax.axis_size("wide")
    n_narrow = lax.axis_size("narrow")
    rows = factor_b.shape[0]
    w = lax.axis_index("wide")
    n = lax.axis_index("narrow")
    x = w // (NY * NC)
    y = (w // NC) % NY
    c = w % NC
    owners = second_ids // TJ_DEV
    inside = second_ids % TJ_DEV

    gram_c = column_gram(factor_c)

    flags = jnp.sum(
        jnp.where(owners[:, None] == jnp.arange(rank, dtype=jnp.int32)[None, :], inside[:, None], 0),
        axis=0,
    )
    flag_rows = jnp.broadcast_to(flags.astype(jnp.bfloat16)[None, :], (16, rank))
    packed = jnp.concatenate([factor_b, flag_rows], axis=0)[None]
    along_x = jnp.concatenate([packed] + [shift_wide(packed, k, 0, 0) for k in (1, 2, 3)], axis=0)
    along_y = jnp.concatenate([along_x] + [shift_wide(along_x, 0, k, 0) for k in (1, 2, 3)], axis=0)
    gathered = jnp.concatenate([along_y, shift_wide(along_y, 0, 0, 1)], axis=0)
    b_rows = gathered[:, :rows]

    def relative(owner):
        ox = owner // (NY * NC)
        oy = (owner // NC) % NY
        oc = owner % NC
        return ((c ^ oc) * NY + (y - oy) % NY) * NX + (x - ox) % NX

    mine = (jnp.arange(rank, dtype=jnp.int32) == w).astype(jnp.float32)
    flags_rel = jnp.sum(gathered[:, rows].astype(jnp.float32) * mine[None, :], axis=1).astype(jnp.int32)
    flags_abs = jnp.take(flags_rel, relative(jnp.arange(n_wide, dtype=jnp.int32)))

    b_pick = relative(owners) * TJ_DEV + inside
    tables = (first_ids, b_pick, depth_ids, count)

    gram_plane = column_gram(b_rows.reshape(n_wide * rows, rank))
    half = rank // NC
    piece = lax.dynamic_slice_in_dim(gram_plane, c * half, half, 0)
    arrived = exchange(piece.reshape(n_narrow, half // n_narrow, rank), "narrow")
    first_part = run_pass(
        pass_one_kernel, 0, tables, local_blocks, gathered, factor_c, n_narrow * TI_DEV, False
    )
    first_part, arrived = lax.optimization_barrier((first_part, arrived))
    mine = spread(jnp.sum(arrived, axis=0), n_narrow, "narrow").reshape(half, rank)
    first_part = run_pass(
        pass_one_kernel, 1, tables, local_blocks, gathered, factor_c, n_narrow * TI_DEV, False,
        first_part,
    )
    other = shift_wide(mine, 0, 0, 1)
    gram_b = jnp.concatenate(
        [jnp.where(c == 0, mine, other), jnp.where(c == 0, other, mine)], axis=0
    )
    received = exchange(first_part.reshape(n_narrow, TI_DEV * bs, rank), "narrow")
    factors = invert(gram_b, gram_c)
    out = jax.ShapeDtypeStruct((rows, rank), jnp.float32)
    a_new, a_half = pl.pallas_call(
        apply_first_kernel, out_shape=(out, jax.ShapeDtypeStruct((rows, rank), jnp.bfloat16))
    )(received, *factors)

    a_all = jnp.stack(
        [a_half]
        + [
            lax.ppermute(a_half, "narrow", [(i, (i + k) % n_narrow) for i in range(n_narrow)])
            for k in range(1, n_narrow)
        ]
    )
    a_pick = ((n - first_ids // TI_DEV) % n_narrow) * TI_DEV + first_ids % TI_DEV

    tables = (a_pick, owners, depth_ids, count)
    gram_w = column_gram(a_all.reshape(n_narrow * rows, rank))
    arrived = exchange(gram_w.reshape(n_wide, rank // n_wide, rank), "wide")
    second_part = run_pass(
        pass_two_kernel, 0, tables, local_blocks, a_all, factor_c, n_wide, True
    )
    second_part, arrived = lax.optimization_barrier((second_part, arrived))
    gram_a = spread(jnp.sum(arrived, axis=0), n_wide, "wide").reshape(rank, rank)
    second_part = run_pass(
        pass_two_kernel, 1, tables, local_blocks, a_all, factor_c, n_wide, True, second_part
    )
    second_part, gram_a = lax.optimization_barrier((second_part, gram_a))
    received_b = exchange(second_part, "wide")
    factors_b = invert(gram_a, gram_c)
    vmem = pl.BlockSpec(memory_space=pltpu.VMEM)
    b_new = pl.pallas_call(
        apply_second_kernel,
        out_shape=out,
        in_specs=[pl.BlockSpec(memory_space=pltpu.SMEM)] + [vmem] * 5,
        out_specs=vmem,
        scratch_shapes=[pltpu.VMEM((TJ_DEV, bs, rank), jnp.float32)],
    )(flags_abs, received_b, *factors_b)
    return (a_new, b_new)


def solution(mesh):
    return jax.shard_map(
        local,
        mesh=mesh,
        in_specs=(
            P("wide", "narrow", None, None, None),
            P("wide", "narrow", None),
            P("wide", "narrow", None),
            P("wide", "narrow", None),
            P("wide", "narrow"),
            P(("wide", "narrow"), None),
            P(),
        ),
        out_specs=(P(("wide", "narrow"), None), P(("wide", "narrow"), None)),
        check_vma=False,
    )
```

```python
import functools

import jax
import jax.numpy as jnp
from jax import lax
from jax.experimental import pallas as pl
from jax.experimental.pallas import tpu as pltpu
from jax.sharding import PartitionSpec as P


TI_DEV = 2
TJ_DEV = 2
NX = 4
NY = 4
NC = 2
HI = lax.Precision.HIGHEST
CHUNK = 8
PANEL = 8
UNROLL = 2
WIRE_SCALE = 32.0


def flat_wide(x, y, c):
    return ((x % NX) * NY + (y % NY)) * NC + c


def shift_wide(v, dx, dy, dc):
    pairs = []
    for x in range(NX):
        for y in range(NY):
            for c in range(NC):
                pairs.append((flat_wide(x, y, c), flat_wide(x + dx, y + dy, c ^ dc)))
    return lax.ppermute(v, "wide", pairs)


def column_gram(matrix):
    return lax.dot_general(
        matrix, matrix, (((0,), (0,)), ((), ())), preferred_element_type=jnp.float32
    )


def begin(previous, out_ref):
    @pl.when(pl.program_id(0) == 0)
    def _():
        out_ref[...] = previous[0][...] if previous else jnp.zeros_like(out_ref)


def mixed_chunk(x_ref, u, k, bs, c_rows):
    part = x_ref[u, :, k * CHUNK * bs:(k + 1) * CHUNK * bs]
    mixed = lax.dot_general(
        part, c_rows, (((0,), (0,)), ((), ())), preferred_element_type=jnp.float32
    )
    return mixed.reshape(CHUNK, bs, mixed.shape[-1])


def pass_one_kernel(first, rows_ref, picks_ref, depth_ref, count_ref, x_ref, c_ref, *rest):
    b_refs = rest[:UNROLL]
    *previous, out_ref = rest[UNROLL:]
    bs = x_ref.shape[1]
    begin(previous, out_ref)
    for u in range(UNROLL):
        slot = first + pl.program_id(0) * UNROLL + u

        @pl.when(slot < count_ref[0])
        def _():
            c_rows = c_ref[pl.ds(pl.multiple_of(depth_ref[slot] * bs, bs), bs), :]
            b_rows = b_refs[u][0].astype(jnp.float32)
            target = rows_ref[slot]
            for k in range(bs // CHUNK):
                mixed = mixed_chunk(x_ref, u, k, bs, c_rows)
                term = jnp.sum(mixed * b_rows[None, :, :], axis=1)
                out_ref[target, k * CHUNK:(k + 1) * CHUNK, :] += term


def pass_two_kernel(first, picks_ref, owners_ref, depth_ref, count_ref, x_ref, c_ref, *rest):
    a_refs = rest[:UNROLL]
    *previous, out_ref = rest[UNROLL:]
    bs = x_ref.shape[1]
    begin(previous, out_ref)
    for u in range(UNROLL):
        slot = first + pl.program_id(0) * UNROLL + u

        @pl.when(slot < count_ref[0])
        def _():
            c_rows = c_ref[pl.ds(pl.multiple_of(depth_ref[slot] * bs, bs), bs), :]
            total = jnp.zeros((bs, c_rows.shape[-1]), jnp.float32)
            for k in range(bs // CHUNK):
                mixed = mixed_chunk(x_ref, u, k, bs, c_rows)
                a_rows = a_refs[u][0, k * CHUNK:(k + 1) * CHUNK, :].astype(jnp.float32)
                total = total + jnp.sum(mixed * a_rows[:, None, :], axis=0)
            out_ref[owners_ref[slot]] = total


def run_pass(kernel, piece, pieces, tables, blocks, tiles, factor_c, out_tiles, use_first, previous=None):
    slots, bs, wide_block = blocks.shape
    rank = factor_c.shape[1]
    steps = slots // pieces // UNROLL
    start = piece * steps
    extra = [] if previous is None else [previous]

    def block_map(s, f, p, d, cnt):
        return (jnp.minimum(s + start, (cnt[0] - 1) // UNROLL), 0, 0)

    def tile_map(u, s, f, p, d, cnt):
        slot = jnp.minimum((s + start) * UNROLL + u, cnt[0] - 1)
        pick = (f if use_first else p)[slot]
        return (pick // TJ_DEV, pick % TJ_DEV, 0)

    whole = pl.BlockSpec((out_tiles, bs, rank), lambda s, f, p, d, cnt: (0, 0, 0))
    return pl.pallas_call(
        functools.partial(kernel, start * UNROLL),
        out_shape=jax.ShapeDtypeStruct((out_tiles, bs, rank), jnp.float32),
        grid_spec=pltpu.PrefetchScalarGridSpec(
            num_scalar_prefetch=4,
            grid=(steps,),
            in_specs=[
                pl.BlockSpec((UNROLL, bs, wide_block), block_map),
                pl.BlockSpec(factor_c.shape, lambda s, f, p, d, cnt: (0, 0)),
            ]
            + [
                pl.BlockSpec((1, bs, rank), functools.partial(tile_map, u)) for u in range(UNROLL)
            ]
            + [whole] * len(extra),
            out_specs=whole,
        ),
        compiler_params=pltpu.CompilerParams(dimension_semantics=("arbitrary",)),
        cost_estimate=pl.CostEstimate(
            flops=steps * UNROLL * wide_block * bs * rank * 2,
            bytes_accessed=steps * UNROLL * bs * wide_block * 2,
            transcendentals=0,
        ),
    )(*tables, blocks, factor_c, *([tiles] * UNROLL), *extra)


def mm(a, b, dims=((1,), (0,))):
    return lax.dot_general(a, b, (dims, ((), ())), precision=HI, preferred_element_type=jnp.float32)


def sweep_negated_inverse(ref):
    n = ref.shape[0]
    lane = lax.broadcasted_iota(jnp.int32, (n, n), 1)
    lane_p = lax.broadcasted_iota(jnp.int32, (PANEL, n), 1)
    sub_p = lax.broadcasted_iota(jnp.int32, (PANEL, n), 0)
    sub_1 = lax.broadcasted_iota(jnp.int32, (PANEL, 1), 0)

    def step(block, carry):
        start = pl.multiple_of(block * PANEL, PANEL)
        a = ref[...]
        panel = ref[pl.ds(start, PANEL), :]
        cols = []
        diag = []
        for j in range(PANEL):
            cols.append(jnp.sum(jnp.where(lane == start + j, a, 0.0), axis=1, keepdims=True))
            diag.append(jnp.sum(jnp.where(lane_p == start + j, panel, 0.0), axis=1, keepdims=True))
        for j in range(PANEL):
            here = lane_p == start + j
            inv = 1.0 / diag[j][j:j + 1]
            row = jnp.where(here[:1], inv, panel[j:j + 1] * inv)
            panel = jnp.where(sub_p == j, row, jnp.where(here, 0.0, panel) - diag[j] * row)
            for m in range(j + 1, PANEL):
                entry = diag[m][j:j + 1] * inv
                diag[m] = jnp.where(sub_1 == j, entry, diag[m] - diag[j] * entry)
        panel = jnp.where((lane_p >= start) & (lane_p < start + PANEL), -panel, panel)
        a = jnp.where((lane >= start) & (lane < start + PANEL), 0.0, a)
        for j in range(PANEL):
            a = a - cols[j] * panel[j:j + 1]
        ref[...] = a
        ref[pl.ds(start, PANEL), :] = panel
        return carry

    lax.fori_loop(0, n // PANEL, step, 0)
    ref[...] = -ref[...]


def unit_scale(gram, gram_c):
    rank = gram.shape[0]
    ids = jnp.arange(rank, dtype=jnp.int32)
    diag = jnp.where(ids[:, None] == ids[None, :], gram * gram_c, 0.0)
    return lax.rsqrt(jnp.sum(diag, axis=0, keepdims=True))


def invert_kernel(g_ref, c_ref, scale_ref, a1_ref, t_ref, s1_ref):
    rank = g_ref.shape[0]
    half = rank // 2
    eye = (
        lax.broadcasted_iota(jnp.int32, (rank, rank), 0)
        == lax.broadcasted_iota(jnp.int32, (rank, rank), 1)
    )
    d_row = scale_ref[...]
    d_col = jnp.sum(jnp.where(eye, d_row, 0.0), axis=1, keepdims=True)
    g = g_ref[...] * c_ref[...] * d_row * d_col
    a1_ref[...] = g[:half, :half]
    sweep_negated_inverse(a1_ref)
    b = g[half:, :half]
    t = mm(b, a1_ref[...])
    t_ref[...] = t
    s1_ref[...] = g[half:, half:] - mm(t, b, ((1,), (1,)))
    sweep_negated_inverse(s1_ref)


def invert(gram, gram_c, scale):
    half = gram.shape[0] // 2
    sq = jax.ShapeDtypeStruct((half, half), jnp.float32)
    parts = pl.pallas_call(
        invert_kernel,
        out_shape=(sq, sq, sq),
        cost_estimate=pl.CostEstimate(flops=10**10, bytes_accessed=10**6, transcendentals=0),
    )(gram, gram_c, scale)
    return (scale, *parts)


def apply_inverse(m, scale_ref, a1_ref, t_ref, s1_ref):
    half = a1_ref.shape[0]
    m1 = m[:, :half]
    z2 = mm(m[:, half:] - mm(m1, t_ref[...], ((1,), (1,))), s1_ref[...])
    z1 = mm(m1, a1_ref[...]) - mm(z2, t_ref[...])
    return jnp.concatenate([z1, z2], axis=1) * scale_ref[...]


def apply_first_kernel(m_ref, scale_ref, a1_ref, t_ref, s1_ref, out_ref, half_ref):
    m = m_ref[0]
    for k in range(1, m_ref.shape[0]):
        m = m + m_ref[k]
    z = apply_inverse(m * scale_ref[...], scale_ref, a1_ref, t_ref, s1_ref)
    out_ref[...] = z
    half_ref[...] = z.astype(jnp.bfloat16)


def apply_second_kernel(flags_ref, m_ref, scale_ref, a1_ref, t_ref, s1_ref, out_ref, acc_ref):
    acc_ref[...] = jnp.zeros_like(acc_ref)

    def step(k, carry):
        acc_ref[flags_ref[k]] += m_ref[k]
        return carry

    lax.fori_loop(0, m_ref.shape[0], step, 0)
    m = acc_ref[...].reshape(out_ref.shape) * (1.0 / WIRE_SCALE)
    out_ref[...] = apply_inverse(m, scale_ref, a1_ref, t_ref, s1_ref)


def exchange(parts, axis):
    return lax.all_to_all(parts, axis, 0, 0, tiled=True)


def roll_blocks(parts, offset):
    stacked = jnp.concatenate(parts + parts, axis=0)
    rows = parts[0].shape[0]
    return lax.dynamic_slice_in_dim(stacked, offset * rows, rows * len(parts), 0)


def gather_slices(piece, x, c):
    parts = [shift_wide(piece, k, 0, 0) for k in (3, 2, 1)] + [piece]
    mine = roll_blocks(parts, (3 - x) % NX)
    other = shift_wide(mine, 0, 0, 1)
    return jnp.concatenate(
        [jnp.where(c == 0, mine, other), jnp.where(c == 0, other, mine)], axis=0
    )


def spread(piece, count, axis):
    return exchange(jnp.broadcast_to(piece[None], (count, *piece.shape)), axis)


def local(blocks, row_tile, col_tile, depth_tile, block_count, factor_b, factor_c):
    local_blocks = blocks[0, 0]
    first_ids = row_tile[0, 0]
    second_ids = col_tile[0, 0]
    depth_ids = depth_tile[0, 0]
    count = block_count[0]
    bs = local_blocks.shape[1]
    rank = factor_c.shape[1]
    n_wide = lax.axis_size("wide")
    n_narrow = lax.axis_size("narrow")
    rows = factor_b.shape[0]
    w = lax.axis_index("wide")
    n = lax.axis_index("narrow")
    x = w // (NY * NC)
    y = (w // NC) % NY
    c = w % NC
    owners = second_ids // TJ_DEV
    inside = second_ids % TJ_DEV

    gram_c = column_gram(factor_c)

    packed = factor_b[None]
    along_x = jnp.concatenate([packed] + [shift_wide(packed, k, 0, 0) for k in (1, 2, 3)], axis=0)
    along_y = jnp.concatenate([along_x] + [shift_wide(along_x, 0, k, 0) for k in (1, 2, 3)], axis=0)
    gathered = jnp.concatenate([along_y, shift_wide(along_y, 0, 0, 1)], axis=0)

    def relative(owner):
        ox = owner // (NY * NC)
        oy = (owner // NC) % NY
        oc = owner % NC
        return ((c ^ oc) * NY + (y - oy) % NY) * NX + (x - ox) % NX

    b_pick = relative(owners) * TJ_DEV + inside
    tables = (first_ids, b_pick, depth_ids, count)

    gram_plane = column_gram(gathered.reshape(n_wide * rows, rank))
    share = rank // n_wide
    quarter = rank // (NC * NX)
    piece = lax.dynamic_slice_in_dim(gram_plane, (c * NX + x) * quarter, quarter, 0)
    arrived = spread(piece, n_narrow, "narrow")
    first_part = run_pass(
        pass_one_kernel, 0, 1, tables, local_blocks, gathered, factor_c, n_narrow * TI_DEV, False
    )
    first_part, arrived = lax.optimization_barrier((first_part, arrived))
    received = exchange(first_part.reshape(n_narrow, TI_DEV * bs, rank), "narrow")
    gram_b = gather_slices(jnp.sum(arrived, axis=0), x, c)
    factors = invert(gram_b, gram_c, unit_scale(gram_b, gram_c))
    out = jax.ShapeDtypeStruct((rows, rank), jnp.float32)
    a_new, a_half = pl.pallas_call(
        apply_first_kernel, out_shape=(out, jax.ShapeDtypeStruct((rows, rank), jnp.bfloat16))
    )(received, *factors)

    a_all = jnp.stack(
        [a_half]
        + [
            lax.ppermute(a_half, "narrow", [(i, (i + k) % n_narrow) for i in range(n_narrow)])
            for k in range(1, n_narrow)
        ]
    )
    a_pick = ((n - first_ids // TI_DEV) % n_narrow) * TI_DEV + first_ids % TI_DEV

    tables = (a_pick, owners, depth_ids, count)
    gram_w = column_gram(a_all.reshape(n_narrow * rows, rank))
    arrived = exchange(gram_w.reshape(n_wide, share, rank), "wide")
    second_part = run_pass(
        pass_two_kernel, 0, 2, tables, local_blocks, a_all, factor_c, n_wide, True
    )
    second_part, arrived = lax.optimization_barrier((second_part, arrived))
    lanes = jnp.arange(rank, dtype=jnp.int32)
    flags = jnp.sum(
        jnp.where(owners[:, None] == lanes[None, :], inside[:, None], 0).astype(jnp.float32), axis=0
    )
    message = jnp.concatenate(
        [jnp.sum(arrived, axis=0), jnp.broadcast_to(flags[None, :], (share, rank))], axis=0
    )
    spread_out = spread(message, n_wide, "wide")
    second_part = run_pass(
        pass_two_kernel, 1, 2, tables, local_blocks, a_all, factor_c, n_wide, True, second_part
    )
    second_part, spread_out = lax.optimization_barrier((second_part, spread_out))
    gram_a = spread_out[:, :share].reshape(rank, rank)
    scale_b = unit_scale(gram_a, gram_c)
    wire = (second_part * (scale_b * WIRE_SCALE)[None]).astype(jnp.float16)
    received_b = exchange(wire, "wide").astype(jnp.float32)
    flags_abs = jnp.sum(
        jnp.where(lanes[None, :] == w, spread_out[:, share], 0.0), axis=1
    ).astype(jnp.int32)
    factors_b = invert(gram_a, gram_c, scale_b)
    vmem = pl.BlockSpec(memory_space=pltpu.VMEM)
    b_new = pl.pallas_call(
        apply_second_kernel,
        out_shape=out,
        in_specs=[pl.BlockSpec(memory_space=pltpu.SMEM)] + [vmem] * 5,
        out_specs=vmem,
        scratch_shapes=[pltpu.VMEM((TJ_DEV, bs, rank), jnp.float32)],
    )(flags_abs, received_b, *factors_b)
    return (a_new, b_new)


def solution(mesh):
    return jax.shard_map(
        local,
        mesh=mesh,
        in_specs=(
            P("wide", "narrow", None, None, None),
            P("wide", "narrow", None),
            P("wide", "narrow", None),
            P("wide", "narrow", None),
            P("wide", "narrow"),
            P(("wide", "narrow"), None),
            P(),
        ),
        out_specs=(P(("wide", "narrow"), None), P(("wide", "narrow"), None)),
        check_vma=False,
    )
```

```python
import functools

import jax
import jax.numpy as jnp
from jax import lax
from jax.experimental import pallas as pl
from jax.experimental.pallas import tpu as pltpu
from jax.sharding import PartitionSpec as P


TI_DEV = 2
TJ_DEV = 2
NX = 4
NY = 4
NC = 2
HI = lax.Precision.HIGHEST
CHUNK = 8
PANEL = 8
UNROLL = 2
WIRE_SCALE = 32.0


def flat_wide(x, y, c):
    return ((x % NX) * NY + (y % NY)) * NC + c


def shift_wide(v, dx, dy, dc):
    pairs = []
    for x in range(NX):
        for y in range(NY):
            for c in range(NC):
                pairs.append((flat_wide(x, y, c), flat_wide(x + dx, y + dy, c ^ dc)))
    return lax.ppermute(v, "wide", pairs)


def column_gram(matrix):
    return lax.dot_general(
        matrix, matrix, (((0,), (0,)), ((), ())), preferred_element_type=jnp.float32
    )


def begin(previous, out_ref):
    @pl.when(pl.program_id(0) == 0)
    def _():
        out_ref[...] = previous[0][...] if previous else jnp.zeros_like(out_ref)


def mixed_chunk(x_ref, u, k, bs, c_rows):
    part = x_ref[u, :, k * CHUNK * bs:(k + 1) * CHUNK * bs]
    mixed = lax.dot_general(
        part, c_rows, (((0,), (0,)), ((), ())), preferred_element_type=jnp.float32
    )
    return mixed.reshape(CHUNK, bs, mixed.shape[-1])


def pass_one_kernel(first, rows_ref, picks_ref, depth_ref, count_ref, x_ref, c_ref, *rest):
    b_refs = rest[:UNROLL]
    *previous, out_ref = rest[UNROLL:]
    bs = x_ref.shape[1]
    begin(previous, out_ref)
    for u in range(UNROLL):
        slot = first + pl.program_id(0) * UNROLL + u

        @pl.when(slot < count_ref[0])
        def _():
            c_rows = c_ref[pl.ds(pl.multiple_of(depth_ref[slot] * bs, bs), bs), :]
            b_rows = b_refs[u][0].astype(jnp.float32)
            target = rows_ref[slot]
            for k in range(bs // CHUNK):
                mixed = mixed_chunk(x_ref, u, k, bs, c_rows)
                term = jnp.sum(mixed * b_rows[None, :, :], axis=1)
                out_ref[target, k * CHUNK:(k + 1) * CHUNK, :] += term


def pass_two_kernel(first, picks_ref, owners_ref, depth_ref, count_ref, x_ref, c_ref, *rest):
    a_refs = rest[:UNROLL]
    *previous, out_ref = rest[UNROLL:]
    bs = x_ref.shape[1]
    begin(previous, out_ref)
    for u in range(UNROLL):
        slot = first + pl.program_id(0) * UNROLL + u

        @pl.when(slot < count_ref[0])
        def _():
            c_rows = c_ref[pl.ds(pl.multiple_of(depth_ref[slot] * bs, bs), bs), :]
            total = jnp.zeros((bs, c_rows.shape[-1]), jnp.float32)
            for k in range(bs // CHUNK):
                mixed = mixed_chunk(x_ref, u, k, bs, c_rows)
                a_rows = a_refs[u][0, k * CHUNK:(k + 1) * CHUNK, :].astype(jnp.float32)
                total = total + jnp.sum(mixed * a_rows[:, None, :], axis=0)
            out_ref[owners_ref[slot]] = total


def run_pass(kernel, piece, pieces, tables, blocks, tiles, factor_c, out_tiles, use_first, previous=None):
    slots, bs, wide_block = blocks.shape
    rank = factor_c.shape[1]
    steps = slots // pieces // UNROLL
    start = piece * steps
    extra = [] if previous is None else [previous]

    def block_map(s, f, p, d, cnt):
        return (jnp.minimum(s + start, (cnt[0] - 1) // UNROLL), 0, 0)

    def tile_map(u, s, f, p, d, cnt):
        slot = jnp.minimum((s + start) * UNROLL + u, cnt[0] - 1)
        pick = (f if use_first else p)[slot]
        return (pick // TJ_DEV, pick % TJ_DEV, 0)

    whole = pl.BlockSpec((out_tiles, bs, rank), lambda s, f, p, d, cnt: (0, 0, 0))
    return pl.pallas_call(
        functools.partial(kernel, start * UNROLL),
        out_shape=jax.ShapeDtypeStruct((out_tiles, bs, rank), jnp.float32),
        grid_spec=pltpu.PrefetchScalarGridSpec(
            num_scalar_prefetch=4,
            grid=(steps,),
            in_specs=[
                pl.BlockSpec((UNROLL, bs, wide_block), block_map),
                pl.BlockSpec(factor_c.shape, lambda s, f, p, d, cnt: (0, 0)),
            ]
            + [
                pl.BlockSpec((1, bs, rank), functools.partial(tile_map, u)) for u in range(UNROLL)
            ]
            + [whole] * len(extra),
            out_specs=whole,
        ),
        compiler_params=pltpu.CompilerParams(dimension_semantics=("arbitrary",)),
        cost_estimate=pl.CostEstimate(
            flops=steps * UNROLL * wide_block * bs * rank * 2,
            bytes_accessed=steps * UNROLL * bs * wide_block * 2,
            transcendentals=0,
        ),
    )(*tables, blocks, factor_c, *([tiles] * UNROLL), *extra)


def mm(a, b, dims=((1,), (0,))):
    return lax.dot_general(a, b, (dims, ((), ())), precision=HI, preferred_element_type=jnp.float32)


def sweep_negated_inverse(ref):
    n = ref.shape[0]
    lane = lax.broadcasted_iota(jnp.int32, (n, n), 1)
    lane_p = lax.broadcasted_iota(jnp.int32, (PANEL, n), 1)
    sub_p = lax.broadcasted_iota(jnp.int32, (PANEL, n), 0)
    sub_1 = lax.broadcasted_iota(jnp.int32, (PANEL, 1), 0)

    def step(block, carry):
        start = pl.multiple_of(block * PANEL, PANEL)
        a = ref[...]
        panel = ref[pl.ds(start, PANEL), :]
        cols = []
        diag = []
        for j in range(PANEL):
            cols.append(jnp.sum(jnp.where(lane == start + j, a, 0.0), axis=1, keepdims=True))
            diag.append(jnp.sum(jnp.where(lane_p == start + j, panel, 0.0), axis=1, keepdims=True))
        for j in range(PANEL):
            here = lane_p == start + j
            inv = 1.0 / diag[j][j:j + 1]
            row = jnp.where(here[:1], inv, panel[j:j + 1] * inv)
            panel = jnp.where(sub_p == j, row, jnp.where(here, 0.0, panel) - diag[j] * row)
            for m in range(j + 1, PANEL):
                entry = diag[m][j:j + 1] * inv
                diag[m] = jnp.where(sub_1 == j, entry, diag[m] - diag[j] * entry)
        panel = jnp.where((lane_p >= start) & (lane_p < start + PANEL), -panel, panel)
        a = jnp.where((lane >= start) & (lane < start + PANEL), 0.0, a)
        for j in range(PANEL):
            a = a - cols[j] * panel[j:j + 1]
        ref[...] = a
        ref[pl.ds(start, PANEL), :] = panel
        return carry

    lax.fori_loop(0, n // PANEL, step, 0)
    ref[...] = -ref[...]


def unit_scale(gram, gram_c):
    rank = gram.shape[0]
    ids = jnp.arange(rank, dtype=jnp.int32)
    diag = jnp.where(ids[:, None] == ids[None, :], gram * gram_c, 0.0)
    return lax.rsqrt(jnp.sum(diag, axis=0, keepdims=True))


def invert_kernel(g_ref, c_ref, scale_ref, out_ref, a1_ref, s1_ref):
    rank = g_ref.shape[0]
    half = rank // 2
    eye = (
        lax.broadcasted_iota(jnp.int32, (rank, rank), 0)
        == lax.broadcasted_iota(jnp.int32, (rank, rank), 1)
    )
    d_row = scale_ref[...]
    d_col = jnp.sum(jnp.where(eye, d_row, 0.0), axis=1, keepdims=True)
    g = g_ref[...] * c_ref[...] * d_row * d_col
    a1_ref[...] = g[:half, :half]
    sweep_negated_inverse(a1_ref)
    b = g[half:, :half]
    t = mm(b, a1_ref[...])
    s1_ref[...] = g[half:, half:] - mm(t, b, ((1,), (1,)))
    sweep_negated_inverse(s1_ref)
    s1 = s1_ref[...]
    low = mm(s1, t)
    d1 = d_row[:, :half]
    d2 = d_row[:, half:]
    out_ref[:half, :half] = (a1_ref[...] + mm(t, low, ((0,), (0,)))) * d1
    out_ref[:half, half:] = -mm(t, s1, ((0,), (0,))) * d2
    out_ref[half:, :half] = -low * d1
    out_ref[half:, half:] = s1 * d2


def invert(gram, gram_c, scale):
    rank = gram.shape[0]
    half = rank // 2
    return pl.pallas_call(
        invert_kernel,
        out_shape=jax.ShapeDtypeStruct((rank, rank), jnp.float32),
        scratch_shapes=[pltpu.VMEM((half, half), jnp.float32)] * 2,
        cost_estimate=pl.CostEstimate(flops=10**10, bytes_accessed=10**6, transcendentals=0),
    )(gram, gram_c, scale)


def apply_first_kernel(m_ref, scale_ref, inverse_ref, out_ref, half_ref):
    z = mm(m_ref[...] * scale_ref[...], inverse_ref[...])
    out_ref[...] = z
    half_ref[...] = z.astype(jnp.bfloat16)


def apply_second_kernel(m_ref, inverse_ref, out_ref):
    out_ref[...] = mm(m_ref[...] * (1.0 / WIRE_SCALE), inverse_ref[...])


def exchange(parts, axis):
    return lax.all_to_all(parts, axis, 0, 0, tiled=True)


def roll_blocks(parts, offset):
    stacked = jnp.concatenate(parts + parts, axis=0)
    rows = parts[0].shape[0]
    return lax.dynamic_slice_in_dim(stacked, offset * rows, rows * len(parts), 0)


def gather_slices(piece, x, c):
    parts = [shift_wide(piece, k, 0, 0) for k in (3, 2, 1)] + [piece]
    mine = roll_blocks(parts, (3 - x) % NX)
    other = shift_wide(mine, 0, 0, 1)
    return jnp.concatenate(
        [jnp.where(c == 0, mine, other), jnp.where(c == 0, other, mine)], axis=0
    )


def spread(piece, count, axis):
    return exchange(jnp.broadcast_to(piece[None], (count, *piece.shape)), axis)


def local(blocks, row_tile, col_tile, depth_tile, block_count, factor_b, factor_c):
    local_blocks = blocks[0, 0]
    first_ids = row_tile[0, 0]
    second_ids = col_tile[0, 0]
    depth_ids = depth_tile[0, 0]
    count = block_count[0]
    bs = local_blocks.shape[1]
    rank = factor_c.shape[1]
    n_wide = lax.axis_size("wide")
    n_narrow = lax.axis_size("narrow")
    rows = factor_b.shape[0]
    w = lax.axis_index("wide")
    n = lax.axis_index("narrow")
    x = w // (NY * NC)
    y = (w // NC) % NY
    c = w % NC
    owners = second_ids // TJ_DEV
    inside = second_ids % TJ_DEV

    gram_c = column_gram(factor_c)

    packed = factor_b[None]
    along_x = jnp.concatenate([packed] + [shift_wide(packed, k, 0, 0) for k in (1, 2, 3)], axis=0)
    back = shift_wide(along_x, 0, 1, 0)
    ahead = shift_wide(along_x, 0, 3, 0)
    middle = [shift_wide(back[:NX // 2], 0, 1, 0), shift_wide(ahead[NX // 2:], 0, 3, 0)]
    along_y = jnp.concatenate([along_x, back, *middle, ahead], axis=0)
    gathered = jnp.concatenate([along_y, shift_wide(along_y, 0, 0, 1)], axis=0)

    def relative(owner):
        ox = owner // (NY * NC)
        oy = (owner // NC) % NY
        oc = owner % NC
        return ((c ^ oc) * NY + (y - oy) % NY) * NX + (x - ox) % NX

    b_pick = relative(owners) * TJ_DEV + inside
    tables = (first_ids, b_pick, depth_ids, count)

    gram_plane = column_gram(gathered.reshape(n_wide * rows, rank))
    share = rank // n_wide
    quarter = rank // (NC * NX)
    piece = lax.dynamic_slice_in_dim(gram_plane, (c * NX + x) * quarter, quarter, 0)
    arrived = spread(piece, n_narrow, "narrow")
    first_part = run_pass(
        pass_one_kernel, 0, 1, tables, local_blocks, gathered, factor_c, n_narrow * TI_DEV, False
    )
    first_part, arrived = lax.optimization_barrier((first_part, arrived))
    received = exchange(first_part.reshape(n_narrow, TI_DEV * bs, rank), "narrow")
    gram_b = gather_slices(jnp.sum(arrived, axis=0), x, c)
    scale_a = unit_scale(gram_b, gram_c)
    inverse_a = invert(gram_b, gram_c, scale_a)
    out = jax.ShapeDtypeStruct((rows, rank), jnp.float32)
    a_new, a_half = pl.pallas_call(
        apply_first_kernel, out_shape=(out, jax.ShapeDtypeStruct((rows, rank), jnp.bfloat16))
    )(jnp.sum(received, axis=0), scale_a, inverse_a)

    def shift_narrow(v, k):
        return lax.ppermute(v, "narrow", [(i, (i + k) % n_narrow) for i in range(n_narrow)])

    back_2, ahead_2 = shift_narrow(a_half, 2), shift_narrow(a_half, -2)
    back_1, ahead_1 = shift_narrow(a_half, 1), shift_narrow(a_half, -1)
    back_34 = shift_narrow(jnp.concatenate([back_1, back_2[:bs]], axis=0), 2)
    ahead_34 = shift_narrow(jnp.concatenate([ahead_1, ahead_2[bs:]], axis=0), -2)
    a_all = jnp.concatenate(
        [a_half, back_1, back_2, back_34, ahead_34[rows:], ahead_34[:rows], ahead_2, ahead_1], axis=0
    ).reshape(n_narrow, rows, rank)
    a_pick = ((n - first_ids // TI_DEV) % n_narrow) * TI_DEV + first_ids % TI_DEV

    tables = (a_pick, owners, depth_ids, count)
    gram_w = column_gram(a_all.reshape(n_narrow * rows, rank))
    arrived = exchange(gram_w.reshape(n_wide, share, rank), "wide")
    second_part = run_pass(
        pass_two_kernel, 0, 2, tables, local_blocks, a_all, factor_c, n_wide, True
    )
    second_part, arrived = lax.optimization_barrier((second_part, arrived))
    lanes = jnp.arange(rank, dtype=jnp.int32)
    flags = jnp.sum(
        jnp.where(owners[:, None] == lanes[None, :], inside[:, None], 0).astype(jnp.float32), axis=0
    )
    message = jnp.concatenate(
        [jnp.sum(arrived, axis=0), jnp.broadcast_to(flags[None, :], (share, rank))], axis=0
    )
    spread_out = spread(message, n_wide, "wide")
    second_part = run_pass(
        pass_two_kernel, 1, 2, tables, local_blocks, a_all, factor_c, n_wide, True, second_part
    )
    second_part, spread_out = lax.optimization_barrier((second_part, spread_out))
    gram_a = spread_out[:, :share].reshape(rank, rank)
    scale_b = unit_scale(gram_a, gram_c)
    wire = (second_part * (scale_b * WIRE_SCALE)[None]).astype(jnp.float16)
    received_b = exchange(wire, "wide").astype(jnp.float32)
    upper = jnp.sum(jnp.where(lanes[None, :] == w, spread_out[:, share], 0.0), axis=1)
    upper = upper[:, None, None] > 0.5
    mttkrp_b = jnp.concatenate(
        [
            jnp.sum(jnp.where(upper, 0.0, received_b), axis=0),
            jnp.sum(jnp.where(upper, received_b, 0.0), axis=0),
        ],
        axis=0,
    )
    inverse_b = invert(gram_a, gram_c, scale_b)
    b_new = pl.pallas_call(apply_second_kernel, out_shape=out)(mttkrp_b, inverse_b)
    return (a_new, b_new)


def solution(mesh):
    return jax.shard_map(
        local,
        mesh=mesh,
        in_specs=(
            P("wide", "narrow", None, None, None),
            P("wide", "narrow", None),
            P("wide", "narrow", None),
            P("wide", "narrow", None),
            P("wide", "narrow"),
            P(("wide", "narrow"), None),
            P(),
        ),
        out_specs=(P(("wide", "narrow"), None), P(("wide", "narrow"), None)),
        check_vma=False,
    )
```

```python
import functools

import jax
import jax.numpy as jnp
from jax import lax
from jax.experimental import pallas as pl
from jax.experimental.pallas import tpu as pltpu
from jax.sharding import PartitionSpec as P


TI_DEV = 2
TJ_DEV = 2
NX = 4
NY = 4
NC = 2
HI = lax.Precision.HIGHEST
CHUNK = 8
PANEL = 8
UNROLL = 2
WIRE_SCALE = 32.0


def flat_wide(x, y, c):
    return ((x % NX) * NY + (y % NY)) * NC + c


def shift_wide(v, dx, dy, dc):
    pairs = []
    for x in range(NX):
        for y in range(NY):
            for c in range(NC):
                pairs.append((flat_wide(x, y, c), flat_wide(x + dx, y + dy, c ^ dc)))
    return lax.ppermute(v, "wide", pairs)


def column_gram(matrix):
    return lax.dot_general(
        matrix, matrix, (((0,), (0,)), ((), ())), preferred_element_type=jnp.float32
    )


def mixed_chunk(x_ref, u, k, bs, c_rows):
    part = x_ref[u, :, k * CHUNK * bs:(k + 1) * CHUNK * bs]
    mixed = lax.dot_general(
        part, c_rows, (((0,), (0,)), ((), ())), preferred_element_type=jnp.float32
    )
    return mixed.reshape(CHUNK, bs, mixed.shape[-1])


def pass_one_kernel(first, rows_ref, picks_ref, depth_ref, count_ref, x_ref, c_ref, *rest):
    b_refs = rest[:UNROLL]
    out_ref = rest[UNROLL]
    bs = x_ref.shape[1]

    @pl.when(pl.program_id(0) == 0)
    def _():
        out_ref[...] = jnp.zeros_like(out_ref)

    for u in range(UNROLL):
        slot = first + pl.program_id(0) * UNROLL + u

        @pl.when(slot < count_ref[0])
        def _():
            c_rows = c_ref[pl.ds(pl.multiple_of(depth_ref[slot] * bs, bs), bs), :]
            b_rows = b_refs[u][0].astype(jnp.float32)
            target = rows_ref[slot]
            for k in range(bs // CHUNK):
                mixed = mixed_chunk(x_ref, u, k, bs, c_rows)
                term = jnp.sum(mixed * b_rows[None, :, :], axis=1)
                out_ref[target, k * CHUNK:(k + 1) * CHUNK, :] += term


def pass_two_kernel(first, picks_ref, owners_ref, depth_ref, count_ref, x_ref, c_ref, *rest):
    a_refs = rest[:UNROLL]
    _, out_ref, tile_ref, sem = rest[UNROLL:]
    bs = x_ref.shape[1]
    step = pl.program_id(0)

    def copy(u, slot):
        return pltpu.make_async_copy(tile_ref.at[u], out_ref.at[owners_ref[slot]], sem.at[u])

    for u in range(UNROLL):
        slot = first + step * UNROLL + u

        @pl.when((step > 0) & (slot - UNROLL < count_ref[0]))
        def _():
            copy(u, slot - UNROLL).wait()

        @pl.when(slot < count_ref[0])
        def _():
            c_rows = c_ref[pl.ds(pl.multiple_of(depth_ref[slot] * bs, bs), bs), :]
            total = jnp.zeros((bs, c_rows.shape[-1]), jnp.float32)
            for k in range(bs // CHUNK):
                mixed = mixed_chunk(x_ref, u, k, bs, c_rows)
                a_rows = a_refs[u][0, k * CHUNK:(k + 1) * CHUNK, :].astype(jnp.float32)
                total = total + jnp.sum(mixed * a_rows[:, None, :], axis=0)
            tile_ref[u] = total
            copy(u, slot).start()

    for u in range(UNROLL):
        slot = first + step * UNROLL + u

        @pl.when((step == pl.num_programs(0) - 1) & (slot < count_ref[0]))
        def _():
            copy(u, slot).wait()


def run_pass(kernel, piece, pieces, tables, blocks, tiles, factor_c, out_tiles, use_first, previous=None):
    slots, bs, wide_block = blocks.shape
    rank = factor_c.shape[1]
    steps = slots // pieces // UNROLL
    start = piece * steps
    extra = [] if previous is None else [previous]
    scratch = []

    def block_map(s, f, p, d, cnt):
        return (jnp.minimum(s + start, (cnt[0] - 1) // UNROLL), 0, 0)

    def tile_map(u, s, f, p, d, cnt):
        slot = jnp.minimum((s + start) * UNROLL + u, cnt[0] - 1)
        pick = (f if use_first else p)[slot]
        return (pick // TJ_DEV, pick % TJ_DEV, 0)

    whole = pl.BlockSpec((out_tiles, bs, rank), lambda s, f, p, d, cnt: (0, 0, 0))
    aliases = {}
    if extra:
        whole = pl.BlockSpec(memory_space=pl.ANY)
        scratch = [pltpu.VMEM((UNROLL, bs, rank), jnp.float32), pltpu.SemaphoreType.DMA((UNROLL,))]
        aliases = {len(tables) + 2 + UNROLL: 0}
    return pl.pallas_call(
        functools.partial(kernel, start * UNROLL),
        out_shape=jax.ShapeDtypeStruct((out_tiles, bs, rank), jnp.float32),
        grid_spec=pltpu.PrefetchScalarGridSpec(
            num_scalar_prefetch=4,
            grid=(steps,),
            in_specs=[
                pl.BlockSpec((UNROLL, bs, wide_block), block_map),
                pl.BlockSpec(factor_c.shape, lambda s, f, p, d, cnt: (0, 0)),
            ]
            + [
                pl.BlockSpec((1, bs, rank), functools.partial(tile_map, u)) for u in range(UNROLL)
            ]
            + [whole] * len(extra),
            out_specs=whole,
            scratch_shapes=scratch,
        ),
        input_output_aliases=aliases,
        compiler_params=pltpu.CompilerParams(dimension_semantics=("arbitrary",)),
        cost_estimate=pl.CostEstimate(
            flops=steps * UNROLL * wide_block * bs * rank * 2,
            bytes_accessed=steps * UNROLL * bs * wide_block * 2,
            transcendentals=0,
        ),
    )(*tables, blocks, factor_c, *([tiles] * UNROLL), *extra)


def mm(a, b, dims=((1,), (0,))):
    return lax.dot_general(a, b, (dims, ((), ())), precision=HI, preferred_element_type=jnp.float32)


def sweep_negated_inverse(ref):
    n = ref.shape[0]
    lane = lax.broadcasted_iota(jnp.int32, (n, n), 1)
    lane_p = lax.broadcasted_iota(jnp.int32, (PANEL, n), 1)
    sub_p = lax.broadcasted_iota(jnp.int32, (PANEL, n), 0)
    sub_1 = lax.broadcasted_iota(jnp.int32, (PANEL, 1), 0)

    def step(block, carry):
        start = pl.multiple_of(block * PANEL, PANEL)
        a = ref[...]
        panel = ref[pl.ds(start, PANEL), :]
        cols = []
        diag = []
        for j in range(PANEL):
            cols.append(jnp.sum(jnp.where(lane == start + j, a, 0.0), axis=1, keepdims=True))
            diag.append(jnp.sum(jnp.where(lane_p == start + j, panel, 0.0), axis=1, keepdims=True))
        for j in range(PANEL):
            here = lane_p == start + j
            inv = 1.0 / diag[j][j:j + 1]
            row = jnp.where(here[:1], inv, panel[j:j + 1] * inv)
            panel = jnp.where(sub_p == j, row, jnp.where(here, 0.0, panel) - diag[j] * row)
            for m in range(j + 1, PANEL):
                entry = diag[m][j:j + 1] * inv
                diag[m] = jnp.where(sub_1 == j, entry, diag[m] - diag[j] * entry)
        panel = jnp.where((lane_p >= start) & (lane_p < start + PANEL), -panel, panel)
        a = jnp.where((lane >= start) & (lane < start + PANEL), 0.0, a)
        for j in range(PANEL):
            a = a - cols[j] * panel[j:j + 1]
        ref[...] = a
        ref[pl.ds(start, PANEL), :] = panel
        return carry

    lax.fori_loop(0, n // PANEL, step, 0)
    ref[...] = -ref[...]


def unit_scale(gram, gram_c):
    rank = gram.shape[0]
    ids = jnp.arange(rank, dtype=jnp.int32)
    diag = jnp.where(ids[:, None] == ids[None, :], gram * gram_c, 0.0)
    return lax.rsqrt(jnp.sum(diag, axis=0, keepdims=True))


def invert_kernel(g_ref, c_ref, scale_ref, out_ref, a1_ref, s1_ref):
    rank = g_ref.shape[0]
    half = rank // 2
    eye = (
        lax.broadcasted_iota(jnp.int32, (rank, rank), 0)
        == lax.broadcasted_iota(jnp.int32, (rank, rank), 1)
    )
    d_row = scale_ref[...]
    d_col = jnp.sum(jnp.where(eye, d_row, 0.0), axis=1, keepdims=True)
    g = g_ref[...] * c_ref[...] * d_row * d_col
    a1_ref[...] = g[:half, :half]
    sweep_negated_inverse(a1_ref)
    b = g[half:, :half]
    t = mm(b, a1_ref[...])
    s1_ref[...] = g[half:, half:] - mm(t, b, ((1,), (1,)))
    sweep_negated_inverse(s1_ref)
    s1 = s1_ref[...]
    low = mm(s1, t)
    d1 = d_row[:, :half]
    d2 = d_row[:, half:]
    out_ref[:half, :half] = (a1_ref[...] + mm(t, low, ((0,), (0,)))) * d1
    out_ref[:half, half:] = -mm(t, s1, ((0,), (0,))) * d2
    out_ref[half:, :half] = -low * d1
    out_ref[half:, half:] = s1 * d2


def invert(gram, gram_c, scale):
    rank = gram.shape[0]
    half = rank // 2
    return pl.pallas_call(
        invert_kernel,
        out_shape=jax.ShapeDtypeStruct((rank, rank), jnp.float32),
        scratch_shapes=[pltpu.VMEM((half, half), jnp.float32)] * 2,
        cost_estimate=pl.CostEstimate(flops=10**10, bytes_accessed=10**6, transcendentals=0),
    )(gram, gram_c, scale)


def apply_first_kernel(m_ref, scale_ref, inverse_ref, out_ref, half_ref):
    z = mm(m_ref[...] * scale_ref[...], inverse_ref[...])
    out_ref[...] = z
    half_ref[...] = z.astype(jnp.bfloat16)


def apply_second_kernel(m_ref, inverse_ref, out_ref):
    out_ref[...] = mm(m_ref[...] * (1.0 / WIRE_SCALE), inverse_ref[...])


def exchange(parts, axis):
    return lax.all_to_all(parts, axis, 0, 0, tiled=True)


def roll_blocks(parts, offset):
    stacked = jnp.concatenate(parts + parts, axis=0)
    rows = parts[0].shape[0]
    return lax.dynamic_slice_in_dim(stacked, offset * rows, rows * len(parts), 0)


def gather_slices(piece, x, c):
    parts = [shift_wide(piece, k, 0, 0) for k in (3, 2, 1)] + [piece]
    mine = roll_blocks(parts, (3 - x) % NX)
    other = shift_wide(mine, 0, 0, 1)
    return jnp.concatenate(
        [jnp.where(c == 0, mine, other), jnp.where(c == 0, other, mine)], axis=0
    )


def spread(piece, count, axis):
    return exchange(jnp.broadcast_to(piece[None], (count, *piece.shape)), axis)


def local(blocks, row_tile, col_tile, depth_tile, block_count, factor_b, factor_c):
    local_blocks = blocks[0, 0]
    first_ids = row_tile[0, 0]
    second_ids = col_tile[0, 0]
    depth_ids = depth_tile[0, 0]
    count = block_count[0]
    bs = local_blocks.shape[1]
    rank = factor_c.shape[1]
    n_wide = lax.axis_size("wide")
    n_narrow = lax.axis_size("narrow")
    rows = factor_b.shape[0]
    w = lax.axis_index("wide")
    n = lax.axis_index("narrow")
    x = w // (NY * NC)
    y = (w // NC) % NY
    c = w % NC
    owners = second_ids // TJ_DEV
    inside = second_ids % TJ_DEV

    gram_c = column_gram(factor_c)

    def relative(owner):
        ox = owner // (NY * NC)
        oy = (owner // NC) % NY
        oc = owner % NC
        return ((c ^ oc) * NY + (y - oy) % NY) * NX + (x - ox) % NX

    packed = factor_b[None]
    along_x = jnp.concatenate([packed] + [shift_wide(packed, k, 0, 0) for k in (1, 2, 3)], axis=0)
    back = shift_wide(along_x, 0, 1, 0)
    ahead = shift_wide(along_x, 0, 3, 0)
    a_pick = ((n - first_ids // TI_DEV) % n_narrow) * TI_DEV + first_ids % TI_DEV
    b_pick = relative(owners) * TJ_DEV + inside
    empty = jnp.full((n_wide, bs, rank), jnp.minimum(count[0], 0), jnp.float32)
    back, a_pick, b_pick, empty = lax.optimization_barrier((back, a_pick, b_pick, empty))
    middle = [shift_wide(back[:NX // 2], 0, 1, 0), shift_wide(ahead[NX // 2:], 0, 3, 0)]
    along_y = jnp.concatenate([along_x, back, *middle, ahead], axis=0)
    gathered = jnp.concatenate([along_y, shift_wide(along_y, 0, 0, 1)], axis=0)

    tables = (first_ids, b_pick, depth_ids, count)

    gram_plane = column_gram(gathered.reshape(n_wide * rows, rank))
    share = rank // n_wide
    quarter = rank // (NC * NX)
    piece = lax.dynamic_slice_in_dim(gram_plane, (c * NX + x) * quarter, quarter, 0)
    arrived = spread(piece, n_narrow, "narrow")
    first_part = run_pass(
        pass_one_kernel, 0, 1, tables, local_blocks, gathered, factor_c, n_narrow * TI_DEV, False
    )
    first_part, arrived = lax.optimization_barrier((first_part, arrived))
    received = exchange(first_part.reshape(n_narrow, TI_DEV * bs, rank), "narrow")
    gram_b = gather_slices(jnp.sum(arrived, axis=0), x, c)
    scale_a = unit_scale(gram_b, gram_c)
    inverse_a = invert(gram_b, gram_c, scale_a)
    out = jax.ShapeDtypeStruct((rows, rank), jnp.float32)
    a_new, a_half = pl.pallas_call(
        apply_first_kernel, out_shape=(out, jax.ShapeDtypeStruct((rows, rank), jnp.bfloat16))
    )(jnp.sum(received, axis=0), scale_a, inverse_a)

    def shift_narrow(v, k):
        return lax.ppermute(v, "narrow", [(i, (i + k) % n_narrow) for i in range(n_narrow)])

    back_2, ahead_2 = shift_narrow(a_half, 2), shift_narrow(a_half, -2)
    back_1, ahead_1 = shift_narrow(a_half, 1), shift_narrow(a_half, -1)
    back_34 = shift_narrow(jnp.concatenate([back_1, back_2[:bs]], axis=0), 2)
    ahead_34 = shift_narrow(jnp.concatenate([ahead_1, ahead_2[bs:]], axis=0), -2)
    a_all = jnp.concatenate(
        [a_half, back_1, back_2, back_34, ahead_34[rows:], ahead_34[:rows], ahead_2, ahead_1], axis=0
    ).reshape(n_narrow, rows, rank)

    tables = (a_pick, owners, depth_ids, count)
    gram_w = column_gram(a_all.reshape(n_narrow * rows, rank))
    arrived = exchange(gram_w.reshape(n_wide, share, rank), "wide")
    second_part = run_pass(
        pass_two_kernel, 0, 2, tables, local_blocks, a_all, factor_c, n_wide, True, empty
    )
    second_part, arrived = lax.optimization_barrier((second_part, arrived))
    lanes = jnp.arange(rank, dtype=jnp.int32)
    flags = jnp.sum(
        jnp.where(owners[:, None] == lanes[None, :], inside[:, None], 0).astype(jnp.float32), axis=0
    )
    message = jnp.concatenate(
        [jnp.sum(arrived, axis=0), jnp.broadcast_to(flags[None, :], (share, rank))], axis=0
    )
    spread_out = spread(message, n_wide, "wide")
    second_part = run_pass(
        pass_two_kernel, 1, 2, tables, local_blocks, a_all, factor_c, n_wide, True, second_part
    )
    second_part, spread_out = lax.optimization_barrier((second_part, spread_out))
    gram_a = spread_out[:, :share].reshape(rank, rank)
    scale_b = unit_scale(gram_a, gram_c)
    wire = (second_part * (scale_b * WIRE_SCALE)[None]).astype(jnp.float16)
    received_b = exchange(wire, "wide").astype(jnp.float32)
    upper = jnp.sum(jnp.where(lanes[None, :] == w, spread_out[:, share], 0.0), axis=1)
    upper = upper[:, None, None] > 0.5
    mttkrp_b = jnp.concatenate(
        [
            jnp.sum(jnp.where(upper, 0.0, received_b), axis=0),
            jnp.sum(jnp.where(upper, received_b, 0.0), axis=0),
        ],
        axis=0,
    )
    inverse_b = invert(gram_a, gram_c, scale_b)
    b_new = pl.pallas_call(apply_second_kernel, out_shape=out)(mttkrp_b, inverse_b)
    return (a_new, b_new)


def solution(mesh):
    return jax.shard_map(
        local,
        mesh=mesh,
        in_specs=(
            P("wide", "narrow", None, None, None),
            P("wide", "narrow", None),
            P("wide", "narrow", None),
            P("wide", "narrow", None),
            P("wide", "narrow"),
            P(("wide", "narrow"), None),
            P(),
        ),
        out_specs=(P(("wide", "narrow"), None), P(("wide", "narrow"), None)),
        check_vma=False,
    )
```
